32 devices in a mesh: row: 2 (over y), col: 4 (over x, core), tm: 4 (over z).
Axes of the slice: x: 2, y: 2, z: 4, core: 2. Of those that a mesh axis runs over, the one named last changes fastest.
Arguments:
- filled_orbitals: bfloat16 [4, 1024, 1024], P('col', 'row', 'tm'), may hold values from -0.1875 to 0.1875
- empty_orbitals: bfloat16 [4, 1024, 3072], P('col', 'row', 'tm'), may hold values from -0.109375 to 0.109375
- filled_depth: bfloat16 [1024], P('tm'), may hold values from 0.019897461 to 2
- empty_depth: bfloat16 [3072], P('tm'), may hold values from 0.019897461 to 2
- time_points: float32 [4], P('tm'), may hold values from 0.05 to 8
- cosine_weights: float32 [4, 4], replicated, may hold values from -3 to 3
Outputs:
- polar_freq: float32 [4, 4, 1024, 4096], P(None, None, ('row', 'tm'), 'col')
The draws below stay inside these ranges and needn't reach their ends.
All inputs are finite; a program needn't handle non-finite values.
Results may differ from the reference program's by a relative error of at most 0.0033.
Values may be sent and summed in bfloat16 or wider, within the bound.
No kernel may reach another device: no remote copies, remote signals or barrier semaphores. Data moves between devices by JAX's collectives and lax.ppermute only.
A program may use at most 128 MiB of HBM per device.

```python
import math
import jax
import jax.numpy as jnp
from jax import lax

NG = 4096
NOCC = 1024
NEMP = 3072
NT = 4
NF = 4
N_COL = 4


def shard_levels(own_key, extent, pieces, low, largest):
    def one(position, blocks):
        steps = jax.random.uniform(jax.random.fold_in(jax.random.fold_in(own_key, 6), position), (blocks,), jnp.float32, low / len(pieces), largest / len(pieces))
        return jnp.repeat(jnp.exp(steps), extent[position] // blocks).reshape((-1,) + (1,) * (len(extent) - position - 1))

    gain = one(*pieces[0])
    for cut in pieces[1:]:
        gain = gain * one(*cut)
    return gain


def normal_values(rng, shape, deviation, reach, cuts=(), kind=jnp.bfloat16):
    loudness = shard_levels(rng, shape, cuts, -0.22, 0.18) if cuts else 1.0
    result = jax.random.normal(rng, shape, jnp.float32) * deviation * loudness
    return jnp.minimum(jnp.maximum(result, -reach), reach).astype(kind)


def setup_inputs(seed: int = 0) -> dict:
    arg_keys = jax.random.split(jax.random.key(seed), 7)
    return {
        "filled_orbitals": normal_values(arg_keys[0], (N_COL, NG // N_COL, NOCC), NOCC ** -0.5, 0.1875, ((0, 4), (1, 2), (2, 4))),
        "empty_orbitals": normal_values(arg_keys[1], (N_COL, NG // N_COL, NEMP), NEMP ** -0.5, 0.109375, ((0, 4), (1, 2), (2, 4))),
        "filled_depth": jnp.clip(jnp.exp(math.log(2.0) - 4.61031033 * jax.random.uniform(arg_keys[2], (NOCC,), jnp.float32) ** shard_levels(arg_keys[2], (NOCC,), ((0, 4),), -0.2, 0.2)), 0.019897461, 2.0).astype(jnp.bfloat16),
        "empty_depth": jnp.clip(jnp.exp(math.log(2.0) - 4.61031033 * jax.random.uniform(arg_keys[3], (NEMP,), jnp.float32) ** shard_levels(arg_keys[3], (NEMP,), ((0, 4),), -0.2, 0.2)), 0.019897461, 2.0).astype(jnp.bfloat16),
        "time_points": jnp.clip(jnp.exp(math.log(8.0) - 5.075174 * jax.random.uniform(arg_keys[4], (NT,), jnp.float32) ** shard_levels(arg_keys[4], (NT,), ((0, 4),), -0.2, 0.2)), 0.05, 8.0),
        "cosine_weights": normal_values(arg_keys[5], (NF, NT), 0.5, 3.0, (), jnp.float32),
    }


def reference(filled_orbitals, empty_orbitals, filled_depth, empty_depth, time_points, cosine_weights):
    phi_filled = filled_orbitals.reshape(NG, NOCC)
    phi_empty = empty_orbitals.reshape(NG, NEMP)
    filled_wide = phi_filled.astype(jnp.float32)
    empty_wide = phi_empty.astype(jnp.float32)
    depth_filled = filled_depth.astype(jnp.float32)
    depth_empty = empty_depth.astype(jnp.float32)

    def one_time(tau_value):
        scaled_filled = (filled_wide * jnp.exp(-depth_filled * tau_value)[None, :]).astype(jnp.bfloat16)
        scaled_empty = (empty_wide * jnp.exp(-depth_empty * tau_value)[None, :]).astype(jnp.bfloat16)
        green_filled = lax.dot_general(filled_wide, scaled_filled.astype(jnp.float32), (((1,), (1,)), ((), ())), precision=lax.Precision.HIGHEST, preferred_element_type=jnp.float32)
        green_empty = lax.dot_general(empty_wide, scaled_empty.astype(jnp.float32), (((1,), (1,)), ((), ())), precision=lax.Precision.HIGHEST, preferred_element_type=jnp.float32)
        return (-(green_filled * green_empty)).astype(jnp.bfloat16)

    polar_time = lax.map(one_time, time_points)
    polar_freq = jnp.einsum("ft,tpq->fpq", cosine_weights, polar_time.astype(jnp.float32), precision=lax.Precision.HIGHEST)
    return polar_freq.reshape(NF, N_COL, NG // N_COL, NG)
```

```python
import functools

import jax
import jax.numpy as jnp
from jax import lax
from jax.experimental import pallas as pl
from jax.experimental.pallas import tpu as pltpu
from jax.sharding import PartitionSpec as P


LANES = 128


def make_plan(n, rows, cols):
    plan, known = [], set()

    def emit(axis, shift, source, target, half=None):
        if target not in known:
            known.add(target)
            plan.append(("move", axis, shift, source, target, half))

    def own(m, k):
        if k == 0:
            known.add(("P", m, 0))
        elif m == 0 or k in (1, n - 1):
            emit("tm", k if k <= n // 2 else k - n, ("S", (k + m) % n), ("P", m, k))
        elif 2 * k == n and 2 * m == n:
            own(m - 1, k + 1)
            own(m + 1, k - 1)
            emit("tm", -1, ("P", m - 1, k + 1), ("P", m, k, 0), 0)
            emit("tm", 1, ("P", (m + 1) % n, k - 1), ("P", m, k, 1), 1)
        elif 2 * k < n or (2 * k == n and 2 * m > n):
            own((m + 1) % n, k - 1)
            emit("tm", 1, ("P", (m + 1) % n, k - 1), ("P", m, k))
        else:
            own(m - 1, k + 1)
            emit("tm", -1, ("P", m - 1, k + 1), ("P", m, k))

    def parts(m, k):
        return [(m, k, 0), (m, k, 1)] if k and 2 * k == n and 2 * m == n else [(m, k)]

    def across(m, k):
        for dy in range(1, rows):
            for part in parts(m, k):
                emit("row", dy, ("P", *part), ("Y", dy, *part))

    def column(d, k):
        if d:
            low = d & 1
            if low and d > 1:
                emit("col", low, ("F", d - low, k), ("F", d, k))
            else:
                emit("col", d, ("P", 0, k), ("F", d, k))

    def kernel(m, dy):
        plan.append(("kernel", m, dy))

    near = sorted(range(1, n), key=lambda k: (min(k, n - k), k))
    late = [m for pair in zip(range(1, n), range(n - 1, 0, -1)) for m in pair]
    late = list(dict.fromkeys(late))
    for k in near:
        own(0, k)
    across(0, 0)
    for d in range(2, cols, 2):
        column(d, 0)
    for k in near:
        plan.append(("move", "tm", k, ("D", 0), ("D", k), None))
    for m in late[:1]:
        for k in (1, n - 1):
            own(m, k)
    for m in late:
        across(m, 0)
    column(1, 0)
    for k in near:
        for d in range(2, cols, 2):
            column(d, k)
        across(0, k)
        if min(k, n - k) == 1 and 2 * k > n:
            for m in late[:2]:
                for j in near:
                    own(m, j)
        column(1, k)
    for m in late:
        for k in (1, n - 1):
            own(m, k)
    for k in [0, *near]:
        for d in range(3, cols, 2):
            column(d, k)
    kernel(0, 0)
    done = [(0, dy) for dy in range(1, rows)]
    ready = []
    for m in late:
        for k in near:
            own(m, k)
        for k in near:
            across(m, k)
        for item in done:
            kernel(*item)
        kernel(m, 0)
        done = ready
        ready = [(m, dy) for dy in range(1, rows)]
    for item in [*done, *ready]:
        kernel(*item)
    return plan


def chunk_kernel(cuts, count, assemble, *refs):
    refs = list(refs)
    place, cosines, scale_o, scale_e = refs[:4]
    pieces = refs[4 : 4 + len(cuts)]
    rest = refs[4 + len(cuts) :]
    freqs, times = cosines.shape
    if assemble:
        blocks, rest = rest[: assemble * count], rest[assemble * count :]
        out, keep_o, keep_e = rest[:3]
        rest = rest[3:]
    else:
        kept_o, kept_e, _, out = rest[:4]
        rest = rest[4:]
    fo, fe, co, ce, so, se, go, ge, ob, piece_sem, first_sem, out_sem = rest
    bo, be = co.shape[1] // count, ce.shape[1] // count
    width = co.shape[0]

    def pair(source, start, size, at, into_o, into_e, sem, i):
        rows = pl.ds(start, size)
        return [
            pltpu.make_async_copy(
                source.at[:, pl.ds(0, bo)],
                into_o.at[rows, pl.ds(at * bo, bo)],
                sem.at[2 * i],
            ),
            pltpu.make_async_copy(
                source.at[:, pl.ds(bo, be)],
                into_e.at[rows, pl.ds(at * be, be)],
                sem.at[2 * i + 1],
            ),
        ]

    loads = []
    for i, (ref, (start, size, at)) in enumerate(zip(pieces, cuts)):
        loads += pair(ref, start, size, at, co, ce, piece_sem, i)
    if assemble:
        firsts = []
        for i, ref in enumerate(blocks):
            d, k = divmod(i, count)
            firsts += pair(ref, d * width, width, k, fo, fe, first_sem, i)
    else:
        firsts = [
            pltpu.make_async_copy(kept_o, fo, first_sem.at[0]),
            pltpu.make_async_copy(kept_e, fe, first_sem.at[1]),
        ]
    for copy in loads + firsts:
        copy.start()
    for copy in loads:
        copy.wait()

    step = 16

    @pl.loop(0, width // step)
    def _(i):
        rows = pl.ds(pl.multiple_of(i * step, step), step)
        for source, scale, into in ((co, scale_o, so), (ce, scale_e, se)):
            wide = source[rows, :].astype(jnp.float32)
            for t in range(times):
                at = pl.ds(pl.multiple_of(t * width + i * step, step), step)
                into[at, :] = (wide * scale[t : t + 1, :]).astype(jnp.bfloat16)

    for copy in firsts:
        copy.wait()
    keeps = []
    if assemble:
        keeps = [
            pltpu.make_async_copy(fo, keep_o, out_sem.at[1]),
            pltpu.make_async_copy(fe, keep_e, out_sem.at[2]),
        ]
        for copy in keeps:
            copy.start()
    contract = (((1,), (1,)), ((), ()))
    go[...] = lax.dot_general(fo[...], so[...], contract, preferred_element_type=jnp.float32)
    ge[...] = lax.dot_general(fe[...], se[...], contract, preferred_element_type=jnp.float32)

    column, z = place[0], place[2]
    weights = [
        [cosines[f, lax.rem(z + times - t, times)] for t in range(times)] for f in range(freqs)
    ]
    tall = 32
    for d in range(fo.shape[0] // width):
        q = jnp.bitwise_xor(column, d)

        @pl.loop(0, width // tall)
        def _(i, d=d, q=q):
            rows = pl.ds(pl.multiple_of(d * width + i * tall, tall), tall)
            into = pl.ds(pl.multiple_of(i * tall, tall), tall)
            totals = [None] * freqs
            for t in range(times):
                lanes = pl.ds(t * width, width)
                polar = (-(go[rows, lanes] * ge[rows, lanes])).astype(jnp.bfloat16)
                polar = polar.astype(jnp.float32)
                for f in range(freqs):
                    term = weights[f][t] * polar
                    totals[f] = term if t == 0 else totals[f] + term
            for f in range(freqs):
                ob[f, q, into, :] = totals[f]

    put = pltpu.make_async_copy(
        ob,
        out.at[:, :, :, pl.ds(pl.multiple_of(place[1] * width, width), width)],
        out_sem.at[0],
    )
    put.start()
    for copy in [*keeps, put]:
        copy.wait()


def chunk_call(place, cosines, scales, pieces, cuts, firsts, out, shape, count):
    width = sum(size for _, size, at in cuts if at == 0)
    freqs, cols, _, _ = shape
    times = cosines.shape[1]
    ko, ke = scales[0].shape[1], scales[1].shape[1]
    assemble = cols if isinstance(firsts, list) else 0
    tile = cols * width
    hbm = pl.BlockSpec(memory_space=pl.ANY)
    smem = pl.BlockSpec(memory_space=pltpu.SMEM)
    vmem = pl.BlockSpec(memory_space=pltpu.VMEM)
    result = jax.ShapeDtypeStruct(shape, jnp.float32)
    operands = [place, cosines, *scales, *pieces]
    in_specs = [smem, smem, vmem, vmem] + [hbm] * len(pieces)
    if assemble:
        operands += firsts
        in_specs += [hbm] * len(firsts)
        out_shape = (
            result,
            jax.ShapeDtypeStruct((tile, ko), jnp.bfloat16),
            jax.ShapeDtypeStruct((tile, ke), jnp.bfloat16),
        )
        out_specs = (hbm, hbm, hbm)
        aliases = {}
    else:
        operands += [*firsts, out]
        in_specs += [hbm] * 3
        out_shape, out_specs = result, hbm
        aliases = {len(operands) - 1: 0}
    return pl.pallas_call(
        functools.partial(chunk_kernel, cuts, count, assemble),
        out_shape=out_shape,
        in_specs=in_specs,
        out_specs=out_specs,
        input_output_aliases=aliases,
        scratch_shapes=[
            pltpu.VMEM((tile, ko), jnp.bfloat16),
            pltpu.VMEM((tile, ke), jnp.bfloat16),
            pltpu.VMEM((width, ko), jnp.bfloat16),
            pltpu.VMEM((width, ke), jnp.bfloat16),
            pltpu.VMEM((times * width, ko), jnp.bfloat16),
            pltpu.VMEM((times * width, ke), jnp.bfloat16),
            pltpu.VMEM((tile, times * width), jnp.float32),
            pltpu.VMEM((tile, times * width), jnp.float32),
            pltpu.VMEM((freqs, cols, width, width), jnp.float32),
            pltpu.SemaphoreType.DMA((2 * len(pieces),)),
            pltpu.SemaphoreType.DMA((2 * assemble * count if assemble else 2,)),
            pltpu.SemaphoreType.DMA((3,)),
        ],
        compiler_params=pltpu.CompilerParams(vmem_limit_bytes=40 * 2**20),
        cost_estimate=pl.CostEstimate(
            flops=2 * tile * times * width * (ko + ke),
            bytes_accessed=2 * (tile + width) * (ko + ke) + 4 * freqs * tile * width,
            transcendentals=0,
        ),
        name="chunk",
    )(*operands)


def streamed(plan, sizes, filled, empty, filled_depth, empty_depth, time_points, cosines):
    n, rows, cols = sizes["tm"], sizes["row"], sizes["col"]
    z, r, c = lax.axis_index("tm"), lax.axis_index("row"), lax.axis_index("col")
    points, bo = filled.shape[1:]
    be = empty.shape[2]
    width = points // n
    shape = (cosines.shape[0], cols, width, rows * points)
    whole = jnp.concatenate([filled[0], empty[0]], axis=1)
    values = {}
    for d in range(n):
        own = lax.dynamic_slice_in_dim(whole, lax.rem(z + d, n) * width, width, 0)
        values["S", d] = values["P", d, 0] = own
    depth = jnp.concatenate([filled_depth, empty_depth]).astype(jnp.float32)
    values["D", 0] = jnp.concatenate([depth, jnp.broadcast_to(time_points, (LANES,))])[None, :]
    perms = {
        "tm": lambda s: [(i, (i + s) % n) for i in range(n)],
        "row": lambda s: [(i, (i + s) % rows) for i in range(rows)],
        "col": lambda s: [(i, i ^ s) for i in range(cols)],
    }
    half = width // 2
    scales = firsts = out = None
    for step in plan:
        if step[0] == "move":
            _, axis, shift, source, target, part = step
            value = values[source]
            if part is not None:
                value = value[part * half : (part + 1) * half]
            values[target] = lax.ppermute(value, axis, perms[axis](shift))
            continue
        _, m, dy = step
        if scales is None:
            stacked = jnp.concatenate([values["D", k] for k in range(n)], axis=0)
            deep, tau = stacked[:, :-LANES], stacked[:, bo + be :][:, :1]
            scales = [
                jnp.exp(-piece.reshape(1, -1) * tau) for piece in (deep[:, :bo], deep[:, bo:])
            ]
            firsts = [
                values["F", d, k] if d else values["P", 0, k]
                for d in range(cols)
                for k in range(n)
            ]
        pieces, cuts = [], []
        for k in range(n):
            key = ("Y", dy, m, k) if dy else ("P", m, k)
            if key in values:
                pieces.append(values[key])
                cuts.append((0, width, k))
            else:
                pieces += [values[(*key, h)] for h in (0, 1)]
                cuts += [(0, half, k), (half, half, k)]
        block = lax.rem(r + rows - dy, rows) * n + lax.rem(z + m, n)
        place = jnp.stack([c, block, z]).astype(jnp.int32)
        result = chunk_call(
            place, cosines, scales, pieces, tuple(cuts), firsts, out, shape, n
        )
        if isinstance(firsts, list):
            out, *firsts = result
            firsts = tuple(firsts)
        else:
            out = result
    return out


def gathered(sizes, filled, empty, filled_depth, empty_depth, time_points, cosines):
    points = filled.shape[1]
    width = points // sizes["tm"]
    z = lax.axis_index("tm")

    def green(orbitals, depths):
        mine = lax.all_gather(orbitals[0], "tm", axis=1, tiled=True)
        depths = lax.all_gather(depths, "tm", axis=0, tiled=True).astype(jnp.float32)
        first = lax.all_gather(
            lax.dynamic_slice_in_dim(mine, z * width, width, 0), "col", axis=0, tiled=True
        )
        second = lax.all_gather(mine, "row", axis=0, tiled=True)

        def at(tau):
            scaled = (second.astype(jnp.float32) * jnp.exp(-depths * tau)[None, :]).astype(
                jnp.bfloat16
            )
            return lax.dot_general(
                first, scaled, (((1,), (1,)), ((), ())), preferred_element_type=jnp.float32
            )

        return at

    taus = lax.all_gather(time_points, "tm", axis=0, tiled=True)
    at_o, at_e = green(filled, filled_depth), green(empty, empty_depth)
    total = 0.0
    for t in range(taus.shape[0]):
        polar = (-(at_o(taus[t]) * at_e(taus[t]))).astype(jnp.bfloat16).astype(jnp.float32)
        total = total + cosines[:, t, None, None] * polar[None]
    return total.reshape(cosines.shape[0], sizes["col"], width, -1)


def solution(mesh):
    sizes = dict(mesh.shape)
    in_specs = (P("col", "row", "tm"), P("col", "row", "tm"), P("tm"), P("tm"), P("tm"), P())
    out_specs = P(None, None, ("row", "tm"), "col")
    plan = make_plan(sizes["tm"], sizes["row"], sizes["col"])

    def on_device(filled, *rest):
        width = filled.shape[1] // sizes["tm"]
        if width % LANES or sizes["col"] & (sizes["col"] - 1):
            return gathered(sizes, filled, *rest)
        return streamed(plan, sizes, filled, *rest)

    return jax.shard_map(
        on_device, mesh=mesh, in_specs=in_specs, out_specs=out_specs, check_vma=False
    )
```

```python
import functools

import jax
import jax.numpy as jnp
from jax import lax
from jax.experimental import pallas as pl
from jax.experimental.pallas import tpu as pltpu
from jax.sharding import PartitionSpec as P


LANES = 128


def make_plan(n, rows, cols):
    plan, known = [], set()
    near = sorted(range(1, n), key=lambda k: (min(k, n - k), k))
    late = [m for pair in zip(range(1, n), range(n - 1, 0, -1)) for m in pair]
    late = list(dict.fromkeys(late))
    ends = near[:2]
    groups = [[0, *ends]] + [[k] for k in near[2:]]

    def emit(axis, shift, source, target):
        if target not in known:
            known.add(target)
            plan.append(("move", axis, shift, source, target))

    def direct(m, k):
        return m == 0 or k in ends

    def own(m, k, dy=None):
        at = (lambda *key: ("Y", dy, *key)) if dy else (lambda *key: ("P", *key))
        start = (lambda d: ("Y", dy, d, 0)) if dy else (lambda d: ("S", d))
        if direct(m, k):
            shift = k if 2 * k <= n else k - n
            emit("tm", shift, start((k + m) % n), at(m, k))
        elif 2 * k < n or (2 * k == n and 2 * m > n):
            own((m + 1) % n, k - 1, dy)
            emit("tm", 1, at((m + 1) % n, k - 1), at(m, k))
        else:
            own(m - 1, k + 1, dy)
            emit("tm", -1, at(m - 1, k + 1), at(m, k))

    def across(m, ks):
        for dy in range(1, rows):
            for k in ks:
                emit("row", dy, ("P", m, k) if k else ("S", m), ("Y", dy, m, k))

    def spread(g, ds):
        for d in ds:
            if d & 1 and d > 1:
                emit("col", 1, ("F", d - 1, g), ("F", d, g))
            else:
                emit("col", d, ("F", 0, g), ("F", d, g))

    def kernel(*chunks):
        plan.append(("kernel", chunks))

    even, odd = range(2, cols, 2), range(3, cols, 2)
    others = range(1, rows)
    for k in near:
        own(0, k)
    for m in late:
        across(m, [0])
    for k in ends:
        own(late[0], k)
    for k in near:
        plan.append(("move", "tm", k, ("D", 0), ("D", k)))
    for g in range(len(groups)):
        spread(g, even)
        for dy in others:
            emit("row", dy, ("F", 0, g), ("Y", dy, "F", g))
        spread(g, [1] if cols > 1 else [])
        if g == 0:
            for m in late[:2]:
                for k in near:
                    own(m, k)
    for g in range(len(groups)):
        spread(g, odd)
    last = late[-1]
    kernel((0, 0))
    across(late[0], near)
    for m in late[2:]:
        for k in reversed(near):
            own(m, k)
    kernel(*[(dy, 0) for dy in others], (0, late[0]))
    for dy in others:
        for k in ends:
            own(last, k, dy)
    for m in late[1:-1]:
        across(m, near)
    kernel((0, late[1]), *[(dy, late[0]) for dy in others])
    across(last, [k for k in near if k not in ends])
    for m in late[1:-1]:
        kernel(*[(dy, m) for dy in others])
    for m in late[2:]:
        kernel((0, m))
    kernel(*[(dy, last) for dy in others])
    return plan, groups


def chunk_kernel(chunks, blocks, count, *refs):
    refs = list(refs)
    place, cosines, scale_o, scale_e = refs[:4]
    used = 1 + max(piece[0] for piece in [*blocks, *(p for c in chunks for p in c)])
    sources, rest = refs[4 : 4 + used], refs[4 + used :]
    freqs, times = cosines.shape
    if blocks:
        out, keep_o, keep_e = rest[:3]
        rest = rest[3:]
    else:
        kept_o, kept_e, _, out = rest[:4]
        rest = rest[4:]
    fo, fe, co, ce, so, se, go, ge, ob, piece_sem, first_sem, out_sem, keep_sem = rest
    bo, be = co.shape[2] // count, ce.shape[2] // count
    width = co.shape[1]
    cols = fo.shape[0] // width

    def pair(piece, into_o, into_e, sem, i):
        source, there, start, size, at = piece
        rows, there = pl.ds(start, size), pl.ds(there, size)
        source = sources[source]
        return [
            pltpu.make_async_copy(
                source.at[there, pl.ds(0, bo)],
                into_o.at[rows, pl.ds(at * bo, bo)],
                sem.at[2 * i],
            ),
            pltpu.make_async_copy(
                source.at[there, pl.ds(bo, be)],
                into_e.at[rows, pl.ds(at * be, be)],
                sem.at[2 * i + 1],
            ),
        ]

    loads = [
        [
            copy
            for i, piece in enumerate(pieces)
            for copy in pair(piece, co.at[j], ce.at[j], piece_sem.at[j], i)
        ]
        for j, pieces in enumerate(chunks)
    ]
    if blocks:
        firsts = [
            copy
            for i, piece in enumerate(blocks)
            for copy in pair(piece, fo, fe, first_sem, i)
        ]
    else:
        firsts = [
            pltpu.make_async_copy(kept_o, fo, first_sem.at[0]),
            pltpu.make_async_copy(kept_e, fe, first_sem.at[1]),
        ]
    for copy in [*loads[0], *firsts, *(c for later in loads[1:] for c in later)]:
        copy.start()

    step, tall = 16, 64
    contract = (((1,), (1,)), ((), ()))
    column, z = place[0], place[1]
    weights = [
        [-cosines[f, lax.rem(z + times - t, times)] for t in range(times)] for f in range(freqs)
    ]
    keeps, puts = [], []
    for j in range(len(chunks)):
        for copy in loads[j]:
            copy.wait()

        @pl.loop(0, width // step)
        def _(i, j=j):
            rows = pl.ds(pl.multiple_of(i * step, step), step)
            for source, scale, into in ((co, scale_o, so), (ce, scale_e, se)):
                wide = source[j, rows, :].astype(jnp.float32)
                for t in range(times):
                    at = pl.ds(pl.multiple_of(t * width + i * step, step), step)
                    into[at, :] = (wide * scale[t : t + 1, :]).astype(jnp.bfloat16)

        if j == 0:
            for copy in firsts:
                copy.wait()
            if blocks:
                keeps = [
                    pltpu.make_async_copy(fo, keep_o, keep_sem.at[0]),
                    pltpu.make_async_copy(fe, keep_e, keep_sem.at[1]),
                ]
                for copy in keeps:
                    copy.start()
        go[...] = lax.dot_general(fo[...], so[...], contract, preferred_element_type=jnp.float32)
        ge[...] = lax.dot_general(fe[...], se[...], contract, preferred_element_type=jnp.float32)
        lane = pl.ds(pl.multiple_of(place[2 + j] * width, width), width)
        for d in range(cols):
            q = jnp.bitwise_xor(column, d)

            @pl.loop(0, width // tall)
            def _(i, d=d, q=q, j=j):
                rows = pl.ds(pl.multiple_of(d * width + i * tall, tall), tall)
                into = pl.ds(pl.multiple_of(i * tall, tall), tall)
                totals = [None] * freqs
                for t in range(times):
                    lanes = pl.ds(t * width, width)
                    polar = (go[rows, lanes] * ge[rows, lanes]).astype(jnp.bfloat16)
                    polar = polar.astype(jnp.float32)
                    for f in range(freqs):
                        term = weights[f][t] * polar
                        totals[f] = term if t == 0 else totals[f] + term
                for f in range(freqs):
                    ob[j, f, d, into, :] = totals[f]

            put = pltpu.make_async_copy(
                ob.at[j, :, d], out.at[:, q, :, lane], out_sem.at[j * cols + d]
            )
            put.start()
            puts.append(put)
    for copy in [*keeps, *puts]:
        copy.wait()


def chunk_call(place, cosines, scales, sources, chunks, blocks, kept, out, shape, count):
    freqs, cols, width, _ = shape
    times = cosines.shape[1]
    ko, ke = scales[0].shape[1], scales[1].shape[1]
    tile = cols * width
    many = len(chunks)
    hbm = pl.BlockSpec(memory_space=pl.ANY)
    smem = pl.BlockSpec(memory_space=pltpu.SMEM)
    vmem = pl.BlockSpec(memory_space=pltpu.VMEM)
    result = jax.ShapeDtypeStruct(shape, jnp.float32)
    operands = [place, cosines, *scales, *sources]
    in_specs = [smem, smem, vmem, vmem] + [hbm] * len(sources)
    if blocks:
        out_shape = (
            result,
            jax.ShapeDtypeStruct((tile, ko), jnp.bfloat16),
            jax.ShapeDtypeStruct((tile, ke), jnp.bfloat16),
        )
        out_specs = (hbm, hbm, hbm)
        aliases = {}
    else:
        operands += [*kept, out]
        in_specs += [hbm] * 3
        out_shape, out_specs = result, hbm
        aliases = {len(operands) - 1: 0}
    return pl.pallas_call(
        functools.partial(chunk_kernel, chunks, blocks, count),
        out_shape=out_shape,
        in_specs=in_specs,
        out_specs=out_specs,
        input_output_aliases=aliases,
        scratch_shapes=[
            pltpu.VMEM((tile, ko), jnp.bfloat16),
            pltpu.VMEM((tile, ke), jnp.bfloat16),
            pltpu.VMEM((many, width, ko), jnp.bfloat16),
            pltpu.VMEM((many, width, ke), jnp.bfloat16),
            pltpu.VMEM((times * width, ko), jnp.bfloat16),
            pltpu.VMEM((times * width, ke), jnp.bfloat16),
            pltpu.VMEM((tile, times * width), jnp.float32),
            pltpu.VMEM((tile, times * width), jnp.float32),
            pltpu.VMEM((many, freqs, cols, width, width), jnp.float32),
            pltpu.SemaphoreType.DMA((many, 2 * count)),
            pltpu.SemaphoreType.DMA((2 * max(1, len(blocks)),)),
            pltpu.SemaphoreType.DMA((many * cols,)),
            pltpu.SemaphoreType.DMA((2,)),
        ],
        compiler_params=pltpu.CompilerParams(vmem_limit_bytes=36 * 2**20),
        cost_estimate=pl.CostEstimate(
            flops=2 * many * tile * times * width * (ko + ke),
            bytes_accessed=2 * (tile + many * width) * (ko + ke) + 4 * many * freqs * tile * width,
            transcendentals=0,
        ),
        name="chunk",
    )(*operands)


def streamed(plan, groups, sizes, filled, empty, filled_depth, empty_depth, time_points, cosines):
    n, rows, cols = sizes["tm"], sizes["row"], sizes["col"]
    z, r, c = lax.axis_index("tm"), lax.axis_index("row"), lax.axis_index("col")
    points, bo = filled.shape[1:]
    be = empty.shape[2]
    width = points // n
    shape = (cosines.shape[0], cols, width, rows * points)
    whole = jnp.concatenate([filled[0], empty[0]], axis=1)
    values = {}
    for d in range(n):
        values["S", d] = lax.dynamic_slice_in_dim(whole, lax.rem(z + d, n) * width, width, 0)
    depth = jnp.concatenate([filled_depth, empty_depth]).astype(jnp.float32)
    values["D", 0] = jnp.concatenate([depth, jnp.broadcast_to(time_points, (LANES,))])[None, :]
    perms = {
        "tm": lambda s: [(i, (i + s) % n) for i in range(n)],
        "row": lambda s: [(i, (i + s) % rows) for i in range(rows)],
        "col": lambda s: [(i, i ^ s) for i in range(cols)],
    }
    home = {k: (g, i) for g, group in enumerate(groups) for i, k in enumerate(group)}

    def lookup(key):
        if key not in values and key[0] == "F" and key[1] == 0:
            parts = [values["P", 0, k] if k else values["S", 0] for k in groups[key[2]]]
            values[key] = parts[0] if len(parts) == 1 else jnp.concatenate(parts, axis=0)
        return values[key]

    def find(dy, m, k):
        if dy and m == 0:
            return lookup(("Y", dy, "F", home[k][0])), home[k][1] * width
        if dy:
            return lookup(("Y", dy, m, k)), 0
        return lookup(("P", m, k) if k else ("S", m)), 0

    scales = kept = out = None
    for step in plan:
        if step[0] == "move":
            _, axis, shift, source, target = step
            values[target] = lax.ppermute(lookup(source), axis, perms[axis](shift))
            continue
        sources = []

        def entry(array, there, row, k):
            for at, other in enumerate(sources):
                if other is array:
                    return (at, there, row, width, k)
            sources.append(array)
            return (len(sources) - 1, there, row, width, k)

        blocks = []
        if scales is None:
            held = [values["D", k] for k in range(n)]
            end = ("F", cols - 1, len(groups) - 1)
            *held, values[end] = lax.optimization_barrier((*held, lookup(end)))
            stacked = jnp.concatenate(held, axis=0)
            deep, tau = stacked[:, : bo + be], stacked[:, bo + be :][:, :1]
            scales = [
                jnp.exp(-piece.reshape(1, -1) * tau) for piece in (deep[:, :bo], deep[:, bo:])
            ]
            for d in range(cols):
                for k in range(n):
                    g, at = home[k]
                    if d:
                        blocks.append(
                            entry(lookup(("F", d, g)), at * width, d * width, k)
                        )
                    else:
                        blocks.append(entry(*find(0, 0, k), 0, k))
        chunks, spots = [], []
        for dy, m in step[1]:
            chunks.append(tuple(entry(*find(dy, m, k), 0, k) for k in range(n)))
            spots.append(lax.rem(r + rows - dy, rows) * n + lax.rem(z + m, n))
        place = jnp.stack([c, z, *spots]).astype(jnp.int32)
        result = chunk_call(
            place, cosines, scales, sources, tuple(chunks), tuple(blocks), kept, out, shape, n
        )
        if blocks:
            out, *kept = result
        else:
            out = result
    return out


def gathered(sizes, filled, empty, filled_depth, empty_depth, time_points, cosines):
    points = filled.shape[1]
    width = points // sizes["tm"]
    z = lax.axis_index("tm")

    def green(orbitals, depths):
        mine = lax.all_gather(orbitals[0], "tm", axis=1, tiled=True)
        depths = lax.all_gather(depths, "tm", axis=0, tiled=True).astype(jnp.float32)
        first = lax.all_gather(
            lax.dynamic_slice_in_dim(mine, z * width, width, 0), "col", axis=0, tiled=True
        )
        second = lax.all_gather(mine, "row", axis=0, tiled=True)

        def at(tau):
            scaled = (second.astype(jnp.float32) * jnp.exp(-depths * tau)[None, :]).astype(
                jnp.bfloat16
            )
            return lax.dot_general(
                first, scaled, (((1,), (1,)), ((), ())), preferred_element_type=jnp.float32
            )

        return at

    taus = lax.all_gather(time_points, "tm", axis=0, tiled=True)
    at_o, at_e = green(filled, filled_depth), green(empty, empty_depth)
    total = 0.0
    for t in range(taus.shape[0]):
        polar = (-(at_o(taus[t]) * at_e(taus[t]))).astype(jnp.bfloat16).astype(jnp.float32)
        total = total + cosines[:, t, None, None] * polar[None]
    return total.reshape(cosines.shape[0], sizes["col"], width, -1)


def solution(mesh):
    sizes = dict(mesh.shape)
    in_specs = (P("col", "row", "tm"), P("col", "row", "tm"), P("tm"), P("tm"), P("tm"), P())
    out_specs = P(None, None, ("row", "tm"), "col")
    plan, groups = make_plan(sizes["tm"], sizes["row"], sizes["col"])

    def on_device(filled, *rest):
        width = filled.shape[1] // sizes["tm"]
        if width % LANES or sizes["col"] & (sizes["col"] - 1):
            return gathered(sizes, filled, *rest)
        return streamed(plan, groups, sizes, filled, *rest)

    return jax.shard_map(
        on_device, mesh=mesh, in_specs=in_specs, out_specs=out_specs, check_vma=False
    )
```

```python
import functools

import jax
import jax.numpy as jnp
from jax import lax
from jax.experimental import pallas as pl
from jax.experimental.pallas import tpu as pltpu
from jax.sharding import PartitionSpec as P


LANES = 128


def make_plan(n, rows, cols):
    plan, known = [], set()
    near = sorted(range(1, n), key=lambda k: (min(k, n - k), k))
    late = [m for pair in zip(range(1, n), range(n - 1, 0, -1)) for m in pair]
    late = list(dict.fromkeys(late))
    last = late[-1]
    ends, rest = near[:2], near[2:]
    even, odd = range(2, cols, 2), range(3, cols, 2)
    others = range(1, rows)

    def move(axis, shift, sources, gives):
        if gives[0] not in known:
            known.update(gives)
            plan.append(("move", axis, shift, tuple(sources), tuple(gives)))

    def straight(k, stages, dys=(0,)):
        shift = k if 2 * k <= n else k - n
        pairs = [(m, dy) for dy in dys for m in stages]
        move(
            "tm",
            shift,
            [("Y", dy, (k + m) % n, 0) if dy else ("S", (k + m) % n) for m, dy in pairs],
            [("Y", dy, m, k) if dy else ("P", m, k) for m, dy in pairs],
        )

    def relay(m, k):
        if ("P", m, k) in known:
            return
        ahead = 2 * k < n or (2 * k == n and 2 * m > n)
        source = ((m + 1) % n, k - 1) if ahead else (m - 1, k + 1)
        if source[0] and source[1] in rest:
            relay(*source)
        move("tm", 1 if ahead else -1, [("P", *source)], [("P", m, k)])

    def across(pieces):
        for dy in others:
            move("row", dy, [("P", *p) for p in pieces], [("Y", dy, *p) for p in pieces])

    def spread(ks, ds):
        for d in ds:
            low = d & 1 if d > 1 else 0
            sources = [("F", d - low, k) if low else ("P", 0, k) for k in ks]
            move("col", low or d, sources, [("F", d, k) for k in ks])

    def kernel(*chunks):
        plan.append(("kernel", chunks))

    for k in near:
        straight(k, [0])
    spread([0], even)
    across([(late[0], 0)])
    for k in near:
        plan.append(("move", "tm", k, (("D", 0),), (("D", k),)))
    spread([0], [1][: cols - 1])
    for m in late[1:]:
        across([(m, 0)])
    for k in ends:
        spread([k], even)
    for k in ends:
        spread([k], [1][: cols - 1])
    for k in ends:
        straight(k, [late[0]])
    across([(0, k) for k in [0, *ends]])
    for k in rest:
        spread([k], even)
        spread([k], [1][: cols - 1])
    for k in rest:
        relay(late[0], k)
    for k in ends:
        straight(k, [late[1]])
    for k in rest:
        relay(late[1], k)
    for k in rest:
        across([(0, k)])
    for k in [0, *near]:
        spread([k], odd)
    for k in ends:
        across([(late[0], k)])
    kernel((0, 0))
    for k in rest:
        across([(late[0], k)])
    for m in late[2:]:
        for k in rest:
            relay(m, k)
        if m != last:
            for k in ends:
                straight(k, [m])
    for k in ends:
        straight(k, [last], [0, *others])
    kernel(*[(dy, 0) for dy in others])
    for m in late[1:-1]:
        for k in near:
            across([(m, k)])
        if m == late[1]:
            kernel(*[(dy, late[0]) for dy in [0, *others]])
    for k in rest:
        across([(last, k)])
    for m in late[1:]:
        kernel(*[(dy, m) for dy in [0, *others]])
    return plan


def chunk_kernel(chunks, blocks, count, *refs):
    refs = list(refs)
    place, cosines, scale_o, scale_e = refs[:4]
    used = 1 + max(piece[0] for piece in [*blocks, *(p for c in chunks for p in c)])
    sources, rest = refs[4 : 4 + used], refs[4 + used :]
    freqs, times = cosines.shape
    if blocks:
        out, keep_o, keep_e = rest[:3]
        rest = rest[3:]
    else:
        kept_o, kept_e, _, out = rest[:4]
        rest = rest[4:]
    fo, fe, co, ce, so, se, go, ge, ob, piece_sem, first_sem, out_sem, keep_sem = rest
    bo, be = co.shape[2] // count, ce.shape[2] // count
    width = co.shape[1]
    cols = fo.shape[0] // width
    column, z = place[0], place[1]

    def pair(piece, into_o, into_e, sem, i):
        source, there, start, size, at = piece
        rows, there = pl.ds(start, size), pl.ds(there, size)
        source = sources[source]
        return [
            pltpu.make_async_copy(
                source.at[there, pl.ds(0, bo)],
                into_o.at[rows, pl.ds(at * bo, bo)],
                sem.at[2 * i],
            ),
            pltpu.make_async_copy(
                source.at[there, pl.ds(bo, be)],
                into_e.at[rows, pl.ds(at * be, be)],
                sem.at[2 * i + 1],
            ),
        ]

    loads = [
        [
            copy
            for i, piece in enumerate(pieces)
            for copy in pair(piece, co.at[j], ce.at[j], piece_sem.at[j], i)
        ]
        for j, pieces in enumerate(chunks)
    ]
    if blocks:
        firsts = [
            copy
            for i, piece in enumerate(blocks)
            for copy in pair(piece, fo, fe, first_sem, i)
        ]
    else:
        firsts = [
            pltpu.make_async_copy(kept_o, fo, first_sem.at[0]),
            pltpu.make_async_copy(kept_e, fe, first_sem.at[1]),
        ]
    for copy in [*loads[0], *firsts, *(c for later in loads[1:] for c in later)]:
        copy.start()

    step, tall = 16, 64
    contract = (((1,), (1,)), ((), ()))
    weights = [
        [-cosines[f, lax.rem(z + times - t, times)] for t in range(times)] for f in range(freqs)
    ]
    keeps, puts = [], []
    for j in range(len(chunks)):
        for copy in loads[j]:
            copy.wait()

        @pl.loop(0, width // step)
        def _(i, j=j):
            rows = pl.ds(pl.multiple_of(i * step, step), step)
            for source, scale, into in ((co, scale_o, so), (ce, scale_e, se)):
                wide = source[j, rows, :].astype(jnp.float32)
                for t in range(times):
                    at = pl.ds(pl.multiple_of(t * width + i * step, step), step)
                    into[at, :] = (wide * scale[t : t + 1, :]).astype(jnp.bfloat16)

        if j == 0:
            for copy in firsts:
                copy.wait()
            if blocks:
                keeps = [
                    pltpu.make_async_copy(fo, keep_o, keep_sem.at[0]),
                    pltpu.make_async_copy(fe, keep_e, keep_sem.at[1]),
                ]
                for copy in keeps:
                    copy.start()
        go[...] = lax.dot_general(fo[...], so[...], contract, preferred_element_type=jnp.float32)
        ge[...] = lax.dot_general(fe[...], se[...], contract, preferred_element_type=jnp.float32)
        lane = pl.ds(pl.multiple_of(place[2 + j] * width, width), width)
        for d in range(cols):
            q = jnp.bitwise_xor(column, d)

            @pl.loop(0, width // tall)
            def _(i, d=d, q=q, j=j):
                rows = pl.ds(pl.multiple_of(d * width + i * tall, tall), tall)
                into = pl.ds(pl.multiple_of(i * tall, tall), tall)
                totals = [None] * freqs
                for t in range(times):
                    lanes = pl.ds(t * width, width)
                    polar = (go[rows, lanes] * ge[rows, lanes]).astype(jnp.bfloat16)
                    polar = polar.astype(jnp.float32)
                    for f in range(freqs):
                        term = weights[f][t] * polar
                        totals[f] = term if t == 0 else totals[f] + term
                for f in range(freqs):
                    ob[j, f, d, into, :] = totals[f]

            put = pltpu.make_async_copy(
                ob.at[j, :, d], out.at[:, q, :, lane], out_sem.at[j * cols + d]
            )
            put.start()
            puts.append(put)
    for copy in [*keeps, *puts]:
        copy.wait()


def chunk_call(place, cosines, scales, sources, chunks, blocks, kept, out, shape, count):
    freqs, cols, width, _ = shape
    times = cosines.shape[1]
    ko, ke = scales[0].shape[1], scales[1].shape[1]
    tile = cols * width
    many = len(chunks)
    hbm = pl.BlockSpec(memory_space=pl.ANY)
    smem = pl.BlockSpec(memory_space=pltpu.SMEM)
    vmem = pl.BlockSpec(memory_space=pltpu.VMEM)
    result = jax.ShapeDtypeStruct(shape, jnp.float32)
    operands = [place, cosines, *scales, *sources]
    in_specs = [smem, smem, vmem, vmem] + [hbm] * len(sources)
    if blocks:
        out_shape = (
            result,
            jax.ShapeDtypeStruct((tile, ko), jnp.bfloat16),
            jax.ShapeDtypeStruct((tile, ke), jnp.bfloat16),
        )
        out_specs = (hbm, hbm, hbm)
        aliases = {}
    else:
        operands += [*kept, out]
        in_specs += [hbm] * 3
        out_shape, out_specs = result, hbm
        aliases = {len(operands) - 1: 0}
    return pl.pallas_call(
        functools.partial(chunk_kernel, chunks, blocks, count),
        out_shape=out_shape,
        in_specs=in_specs,
        out_specs=out_specs,
        input_output_aliases=aliases,
        scratch_shapes=[
            pltpu.VMEM((tile, ko), jnp.bfloat16),
            pltpu.VMEM((tile, ke), jnp.bfloat16),
            pltpu.VMEM((many, width, ko), jnp.bfloat16),
            pltpu.VMEM((many, width, ke), jnp.bfloat16),
            pltpu.VMEM((times * width, ko), jnp.bfloat16),
            pltpu.VMEM((times * width, ke), jnp.bfloat16),
            pltpu.VMEM((tile, times * width), jnp.float32),
            pltpu.VMEM((tile, times * width), jnp.float32),
            pltpu.VMEM((many, freqs, cols, width, width), jnp.float32),
            pltpu.SemaphoreType.DMA((many, 2 * count)),
            pltpu.SemaphoreType.DMA((2 * max(1, len(blocks)),)),
            pltpu.SemaphoreType.DMA((many * cols,)),
            pltpu.SemaphoreType.DMA((2,)),
        ],
        compiler_params=pltpu.CompilerParams(vmem_limit_bytes=36 * 2**20),
        cost_estimate=pl.CostEstimate(
            flops=2 * many * tile * times * width * (ko + ke),
            bytes_accessed=2 * (tile + many * width) * (ko + ke) + 4 * many * freqs * tile * width,
            transcendentals=0,
        ),
        name="chunk",
    )(*operands)


def streamed(plan, sizes, filled, empty, filled_depth, empty_depth, time_points, cosines):
    n, rows, cols = sizes["tm"], sizes["row"], sizes["col"]
    z, r, c = lax.axis_index("tm"), lax.axis_index("row"), lax.axis_index("col")
    points, bo = filled.shape[1:]
    be = empty.shape[2]
    width = points // n
    shape = (cosines.shape[0], cols, width, rows * points)
    whole = jnp.concatenate([filled[0], empty[0]], axis=1)
    held, joined = {}, {}
    for d in range(n):
        own = lax.dynamic_slice_in_dim(whole, lax.rem(z + d, n) * width, width, 0)
        held["S", d] = held["P", d, 0] = (own, 0)
    depth = jnp.concatenate([filled_depth, empty_depth]).astype(jnp.float32)
    depth = jnp.concatenate([depth, jnp.broadcast_to(time_points, (LANES,))])[None, :]
    held["D", 0] = (depth, 0)
    perms = {
        "tm": lambda s: [(i, (i + s) % n) for i in range(n)],
        "row": lambda s: [(i, (i + s) % rows) for i in range(rows)],
        "col": lambda s: [(i, i ^ s) for i in range(cols)],
    }

    result = [None]

    def after(array):
        if result[0] is not None:
            array, result[0] = lax.optimization_barrier((array, result[0]))
        return array

    def join(keys):
        if keys not in joined:
            array, _ = held[keys[0]]
            spots = [held[key] for key in keys]
            in_place = [spot[0] is array and spot[1] == i * width for i, spot in enumerate(spots)]
            if all(in_place) and array.shape[0] <= len(keys) * width:
                joined[keys] = array
            else:
                parts = [
                    a if a.shape[0] == width else lax.slice_in_dim(after(a), at, at + width)
                    for a, at in spots
                ]
                joined[keys] = parts[0] if len(parts) == 1 else jnp.concatenate(parts, axis=0)
        return joined[keys]

    scales = kept = None
    for step in plan:
        if step[0] == "move":
            _, axis, shift, keys, gives = step
            moved = lax.ppermute(join(keys), axis, perms[axis](shift))
            for at, key in enumerate(gives):
                held[key] = (moved, at * width)
            continue
        sources = []

        def entry(key, row, k):
            array, there = held[key]
            for at, other in enumerate(sources):
                if other is array:
                    return (at, there, row, width, k)
            sources.append(array)
            return (len(sources) - 1, there, row, width, k)

        blocks = []
        if scales is None:
            stacked = [held["D", k][0] for k in range(n)]
            end = ("F", cols - 1, n // 2)
            *stacked, array = lax.optimization_barrier((*stacked, held[end][0]))
            held[end] = (array, held[end][1])
            stacked = jnp.concatenate(stacked, axis=0)
            deep, tau = stacked[:, : bo + be], stacked[:, bo + be :][:, :1]
            scales = [
                jnp.exp(-piece.reshape(1, -1) * tau) for piece in (deep[:, :bo], deep[:, bo:])
            ]
            for d in range(cols):
                for k in range(n):
                    key = ("F", d, k) if d else ("P", 0, k)
                    blocks.append(entry(key, d * width, k))
        chunks, spots = [], []
        for dy, m in step[1]:
            keys = [("Y", dy, m, k) if dy else ("P", m, k) for k in range(n)]
            chunks.append(tuple(entry(key, 0, k) for k, key in enumerate(keys)))
            spots.append(lax.rem(r + rows - dy, rows) * n + lax.rem(z + m, n))
        place = jnp.stack([c, z, *spots]).astype(jnp.int32)
        done = chunk_call(
            place,
            cosines,
            scales,
            sources,
            tuple(chunks),
            tuple(blocks),
            kept,
            result[0],
            shape,
            n,
        )
        if blocks:
            done, *kept = done
        result[0] = done
    return result[0]


def gathered(sizes, filled, empty, filled_depth, empty_depth, time_points, cosines):
    points = filled.shape[1]
    width = points // sizes["tm"]
    z = lax.axis_index("tm")

    def green(orbitals, depths):
        mine = lax.all_gather(orbitals[0], "tm", axis=1, tiled=True)
        depths = lax.all_gather(depths, "tm", axis=0, tiled=True).astype(jnp.float32)
        first = lax.all_gather(
            lax.dynamic_slice_in_dim(mine, z * width, width, 0), "col", axis=0, tiled=True
        )
        second = lax.all_gather(mine, "row", axis=0, tiled=True)

        def at(tau):
            scaled = (second.astype(jnp.float32) * jnp.exp(-depths * tau)[None, :]).astype(
                jnp.bfloat16
            )
            return lax.dot_general(
                first, scaled, (((1,), (1,)), ((), ())), preferred_element_type=jnp.float32
            )

        return at

    taus = lax.all_gather(time_points, "tm", axis=0, tiled=True)
    at_o, at_e = green(filled, filled_depth), green(empty, empty_depth)
    total = 0.0
    for t in range(taus.shape[0]):
        polar = (-(at_o(taus[t]) * at_e(taus[t]))).astype(jnp.bfloat16).astype(jnp.float32)
        total = total + cosines[:, t, None, None] * polar[None]
    return total.reshape(cosines.shape[0], sizes["col"], width, -1)


def solution(mesh):
    sizes = dict(mesh.shape)
    in_specs = (P("col", "row", "tm"), P("col", "row", "tm"), P("tm"), P("tm"), P("tm"), P())
    out_specs = P(None, None, ("row", "tm"), "col")
    plan = make_plan(sizes["tm"], sizes["row"], sizes["col"])

    def on_device(filled, *rest):
        width = filled.shape[1] // sizes["tm"]
        if width % LANES or sizes["tm"] % 2 or sizes["tm"] < 4 or sizes["col"] not in (2, 4):
            return gathered(sizes, filled, *rest)
        return streamed(plan, sizes, filled, *rest)

    return jax.shard_map(
        on_device, mesh=mesh, in_specs=in_specs, out_specs=out_specs, check_vma=False
    )
```
